256 devices in a mesh: gx: 4 (over y), gy: 8 (over z_hi, core), gz: 8 (over z_lo, x).
Axes of the slice: x: 4, y: 4, z: 8 (z_hi: 4, z_lo: 2; z = z_hi * 2 + z_lo), core: 2. Of those that a mesh axis runs over, the one named last changes fastest.
Arguments:
- interior_inverse: bfloat16 [2048, 512, 512], P(('gx', 'gy', 'gz')), may hold values from -0.25 to 0.25
- interior_to_face: bfloat16 [2048, 512, 384], P(('gx', 'gy', 'gz')), may hold values from -0.25 to 0.25
- face_to_interior: bfloat16 [2048, 384, 512], P(('gx', 'gy', 'gz')), may hold values from -6 to 6
- face_diag: bfloat16 [2048, 6, 4096], P(('gx', 'gy', 'gz')), may hold values from -6 to 6
- element_cell: int32 [2048], P(('gx', 'gy', 'gz')), may hold values from 0 to 7, as said below
- face_orient: int32 [2048, 6], P(('gx', 'gy', 'gz')), may hold values from 0 to 7
- face_owner: int32 [8, 16, 16, 3], P('gx', 'gy', 'gz'), may hold values from 0 to 23, as said below
- prescribed_face_mask: int32 [8, 16, 16, 3], P('gx', 'gy', 'gz'), may hold values 0 or 1
Outputs:
- trace_rows: bfloat16 [4, 8, 192, 11, 4096], P('gx', 'gy', 'gz')
The draws below stay inside these ranges and needn't reach their ends.
Inputs may be any that keep to these rules, and one draw needn't show every extreme that they name: `element_cell`: on each device the 8 entries are a permutation of 0 to 7. `face_owner`: within each device's block of 2 x 2 x 2 x 3 entries every value of 0 to 23 appears once.
All inputs are finite; a program needn't handle non-finite values. No bound on the sum of `prescribed_face_mask` on one device may be relied on, other than what follows from the above.
Results may differ from the reference program's by a relative error of at most 0.0052.
Values may be sent and summed in bfloat16 or wider, within the bound.
A program may use at most 128 MiB of HBM per device.

```python
import jax
import jax.numpy as jnp
from jax import lax

Q = 8
NFACE = 64
NINT = 512
EX = 2
EY = 2
ELEMENTS_Z_PART = 2
E_DEV = 8
F_DEV = 24
PER = 3
ELEMS = 2048
ELEMENTS_FIRST = 8
ELEMENTS_SECOND = 16
ELEMENTS_THIRD = 16
N_GX = 4
N_GY = 8
N_GZ = 8


def draw_element_cell(key, part):
    blocks = ELEMS // (EX * EY * ELEMENTS_Z_PART)
    subkeys = jax.random.split(jax.random.fold_in(key, 11), blocks)

    def one_block(block_key):
        return jax.random.permutation(block_key, EX * EY * ELEMENTS_Z_PART)
    ordering_list = jax.vmap(one_block)(subkeys)
    return ordering_list.reshape(ELEMS).astype(jnp.int32)


def draw_face_owner(key, part):
    along_x = ELEMENTS_FIRST // EX
    along_y = ELEMENTS_SECOND // EY
    third_axis_step = ELEMENTS_THIRD // ELEMENTS_Z_PART
    subkeys = jax.random.split(jax.random.fold_in(key, 23), along_x * along_y * third_axis_step)

    def one_block(block_key):
        return jax.random.permutation(block_key, 3 * EX * EY * ELEMENTS_Z_PART)
    ordering_list = jax.vmap(one_block)(subkeys)
    ordering_list = ordering_list.reshape(along_x, along_y, third_axis_step, EX, EY, ELEMENTS_Z_PART, 3)
    ordering_list = jnp.transpose(ordering_list, (0, 3, 1, 4, 2, 5, 6))
    return ordering_list.reshape(ELEMENTS_FIRST, ELEMENTS_SECOND, ELEMENTS_THIRD, 3).astype(jnp.int32)


def touch_ends(result, key, smallest, top_value):
    shape = result.shape
    index_at = [jax.random.randint(jax.random.fold_in(key, axis), (), 0, shape[axis]) for axis in range(len(shape))]
    result = result.at[tuple(index_at)].set(smallest)
    longest = shape.index(max(shape))
    index_at[longest] = (index_at[longest] + 1) % shape[longest]
    return result.at[tuple(index_at)].set(top_value)


def block_scale(key, dims, cuts, smallest, high):
    gain = 1.0
    for axis_at, shards_of in cuts:
        draws = jax.random.uniform(jax.random.fold_in(jax.random.fold_in(key, 6), axis_at), (shards_of,), jnp.float32, smallest / len(cuts), high / len(cuts))
        gain = gain * jnp.repeat(jnp.exp(draws), dims[axis_at] // shards_of).reshape((-1,) + (1,) * (len(dims) - 1 - axis_at))
    return gain


def gaussian(own_key, extent, deviation, most, shards=(), kind=jnp.bfloat16):
    drawn = deviation * jax.random.normal(own_key, extent, jnp.float32)
    if shards:
        drawn = drawn * block_scale(own_key, extent, shards, -0.22, 0.18)
    return jnp.clip(drawn, -most, most).astype(kind)


def setup_inputs(seed: int = 0) -> dict:
    arg_keys = jax.random.split(jax.random.key(seed), 9)
    return {
        "interior_inverse": gaussian(arg_keys[0], (ELEMS, NINT, NINT), NINT ** -0.5, 0.25, ((0, 256),)),
        "interior_to_face": gaussian(arg_keys[1], (ELEMS, NINT, 6 * NFACE), NINT ** -0.5, 0.25, ((0, 256),)),
        "face_to_interior": gaussian(arg_keys[2], (ELEMS, 6 * NFACE, NINT), 1.0, 6.0, ((0, 256),)),
        "face_diag": gaussian(arg_keys[3], (ELEMS, 6, NFACE * NFACE), 1.0, 6.0, ((0, 256),)),
        "element_cell": draw_element_cell(jax.random.fold_in(arg_keys[8], 71), 0),
        "face_orient": touch_ends(jax.random.randint(arg_keys[5], (ELEMS, 6), 0, 8), jax.random.fold_in(arg_keys[5], 1), 0, 7).astype(jnp.int32),
        "face_owner": draw_face_owner(jax.random.fold_in(arg_keys[8], 71), 0),
        "prescribed_face_mask": touch_ends((jax.random.randint(arg_keys[7], (ELEMENTS_FIRST, ELEMENTS_SECOND, ELEMENTS_THIRD, 3), 0, 4) < 1).astype(jnp.int32), jax.random.fold_in(arg_keys[7], 1), 0, 1),
    }


def orientation_map(codes):
    nodes = jnp.arange(NFACE, dtype=jnp.int32)
    first = nodes // Q
    second = nodes % Q
    codes = codes[..., None]
    swapped = (codes // 4) % 2 == 1
    new_first = jnp.where(swapped, second, first)
    new_second = jnp.where(swapped, first, second)
    new_first = jnp.where(codes % 2 == 1, Q - 1 - new_first, new_first)
    new_second = jnp.where((codes // 2) % 2 == 1, Q - 1 - new_second, new_second)
    return (Q * new_first + new_second).astype(jnp.int32)


def schur_blocks(inverse, to_face, to_interior, diagonal_blocks):
    number = inverse.shape[0]
    solved = jnp.einsum('eij,ejk->eik', inverse.astype(jnp.float32), to_face.astype(jnp.float32),
                        precision=lax.Precision.HIGHEST).astype(jnp.bfloat16)
    coupled = jnp.einsum('eij,ejk->eik', to_interior.astype(jnp.float32), solved.astype(jnp.float32),
                         precision=lax.Precision.HIGHEST)
    blocks = -coupled.reshape(number, 6, NFACE, 6, NFACE)
    eye_six = jnp.eye(6, dtype=jnp.float32)
    own = diagonal_blocks.astype(jnp.float32).reshape(number, 6, NFACE, NFACE)
    return blocks + own[:, :, :, None, :] * eye_six[None, :, None, :, None]


def oriented_blocks(blocks, codes):
    number = blocks.shape[0]
    targets = orientation_map(codes)
    slots = jnp.arange(NFACE, dtype=jnp.int32)
    moves = (targets[:, :, None, :] == slots[None, None, :, None]).astype(blocks.dtype)
    turned = jnp.einsum('earn,eanbm,ebsm->eabrs', moves, blocks, moves, precision=lax.Precision.HIGHEST)
    return turned.astype(jnp.bfloat16).reshape(number, 6, 6, NFACE * NFACE)


def identity_row():
    first = jnp.eye(NFACE, dtype=jnp.float32).reshape(1, NFACE * NFACE)
    rest = jnp.zeros((10, NFACE * NFACE), jnp.float32)
    return jnp.concatenate([first, rest], axis=0).astype(jnp.bfloat16)


def assemble(left_all, right_all, direction, flags):
    upper = 2 * direction + 1
    lower = 2 * direction
    diagonal = (left_all[:, :, :, upper].astype(jnp.float32)
                + right_all[:, :, :, lower].astype(jnp.float32)).astype(jnp.bfloat16)
    row = jnp.concatenate([diagonal[:, :, :, None], left_all[:, :, :, :upper], left_all[:, :, :, upper + 1:],
                           right_all[:, :, :, :lower], right_all[:, :, :, lower + 1:]], axis=3)
    marked = flags[:, :, :, direction][:, :, :, None, None] == 1
    return jnp.where(marked, identity_row()[None, None, None], row)


def reference(interior_inverse, interior_to_face, face_to_interior, face_diag, element_cell, face_orient,
              face_owner, prescribed_face_mask):
    devices = N_GX * N_GY * N_GZ
    squared_value = NFACE * NFACE

    def per_device(items):
        inverse, to_face, to_interior, diagonal_blocks, codes = items
        return oriented_blocks(schur_blocks(inverse, to_face, to_interior, diagonal_blocks), codes)

    contrib = lax.map(per_device, (interior_inverse.reshape(devices, E_DEV, NINT, NINT),
                                   interior_to_face.reshape(devices, E_DEV, NINT, 6 * NFACE),
                                   face_to_interior.reshape(devices, E_DEV, 6 * NFACE, NINT),
                                   face_diag.reshape(devices, E_DEV, 6, squared_value),
                                   face_orient.reshape(devices, E_DEV, 6)))
    order = jnp.argsort(element_cell.reshape(devices, E_DEV), axis=1).astype(jnp.int32)
    contrib = jnp.take_along_axis(contrib, order[:, :, None, None, None], axis=1)
    element_lattice = contrib.reshape(N_GX, N_GY, N_GZ, EX, EY, ELEMENTS_Z_PART, 6, 6, squared_value)
    element_lattice = jnp.transpose(element_lattice, (0, 3, 1, 4, 2, 5, 6, 7, 8)).reshape(ELEMENTS_FIRST, ELEMENTS_SECOND, ELEMENTS_THIRD, 6, 6, squared_value)
    row_list = []
    for direction in range(3):
        left_all = element_lattice[:, :, :, 2 * direction + 1]
        right_all = jnp.roll(element_lattice[:, :, :, 2 * direction], -1, axis=direction)
        row_list.append(assemble(left_all, right_all, direction, prescribed_face_mask))
    rows = jnp.stack(row_list, axis=3)
    rows = rows.reshape(N_GX, EX, N_GY, EY, N_GZ, ELEMENTS_Z_PART, 3, 11, squared_value)
    rows = jnp.transpose(rows, (0, 2, 4, 1, 3, 5, 6, 7, 8)).reshape(N_GX, N_GY, N_GZ * F_DEV, 11, squared_value)
    owners = face_owner.reshape(N_GX, EX, N_GY, EY, N_GZ, ELEMENTS_Z_PART, 3)
    owners = jnp.transpose(owners, (0, 2, 4, 1, 3, 5, 6)).reshape(N_GX, N_GY, N_GZ, F_DEV)
    source = jnp.arange(N_GZ, dtype=jnp.int32)[None, None, :, None]
    target = (owners // PER) * F_DEV + source * PER + owners % PER
    target = target.reshape(N_GX, N_GY, N_GZ * F_DEV).astype(jnp.int32)

    def place(values, where):
        return jnp.zeros_like(values).at[where].set(values)

    return jax.vmap(jax.vmap(place))(rows, target)
```

```python
import jax
import jax.numpy as jnp
from jax import lax
from jax.experimental import pallas as pl
from jax.experimental.pallas import tpu as pltpu
from jax.sharding import PartitionSpec as P

Q = 8
NFACE = 64
NINT = 512
FACES = 6
WIDTH = FACES * NFACE
E_DEV = 8
F_DEV = 24
PER = 3
HALF = 32
LANES = 128
MESH = pl.DeviceIdType.MESH
F32 = jnp.float32
BF16 = jnp.bfloat16


def iota(shape, axis):
    return lax.broadcasted_iota(jnp.int32, shape, axis)


def mapped_nodes(nodes, codes):
    first, second = nodes // Q, nodes % Q
    swapped = codes // 4 % 2 == 1
    new_first = jnp.where(swapped, second, first)
    new_second = jnp.where(swapped, first, second)
    new_first = jnp.where(codes % 2 == 1, Q - 1 - new_first, new_first)
    new_second = jnp.where(codes // 2 % 2 == 1, Q - 1 - new_second, new_second)
    return Q * new_first + new_second


def condense_kernel(
    cell_ref,
    orient_ref,
    owner_ref,
    inverse_ref,
    to_face_ref,
    to_interior_ref,
    diag_ref,
    contrib_ref,
    slot_ref,
    diag_rows,
):
    e = pl.program_id(0)

    @pl.when(e == 0)
    def _():
        for f in range(F_DEV):
            slot_ref[owner_ref[f // 12, f // 6 % 2, f // 3 % 2, f % 3]] = f

    diag = diag_ref[0].astype(F32)
    for r in range(HALF):
        diag_rows[pl.ds(r, FACES, stride=HALF), :] = diag[:, r * LANES : (r + 1) * LANES]

    solved = jnp.dot(inverse_ref[0], to_face_ref[0], preferred_element_type=F32).astype(BF16)

    lane = iota((1, LANES), 1)
    row = iota((LANES, LANES), 0)
    col = iota((LANES, LANES), 1)
    row_node = 2 * (row % HALF) + row // HALF % 2 + NFACE * (row // NFACE)
    wide = iota((2 * LANES, LANES), 0)
    wide_node = wide % NFACE + NFACE * (wide // LANES)
    half_nodes = 2 * (lane % HALF) + lane // NFACE
    same_face = row // NFACE == col // NFACE
    low = col < NFACE

    turned_rows = []
    col_moves = []
    own = []
    for p in range(3):
        code_a, code_b = orient_ref[e, 2 * p], orient_ref[e, 2 * p + 1]
        second = lane // NFACE
        codes = jnp.where(second == 1, code_b, code_a)
        target = mapped_nodes(lane % NFACE, codes) + NFACE * second
        row_move = (target == row_node).astype(BF16)
        col_moves.append((target == wide_node).astype(BF16))
        face_rows = to_interior_ref[0, p * LANES : (p + 1) * LANES, :]
        turned_rows.append(jnp.dot(row_move, face_rows, preferred_element_type=F32).astype(BF16))
        second = lane // HALF % 2
        codes = jnp.where(second == 1, code_b, code_a)
        target = mapped_nodes(half_nodes, codes) + NFACE * second
        move = (target == row_node).astype(BF16)
        pair = diag_rows[p * NFACE : (p + 1) * NFACE, :]
        low_pair = low[:NFACE]
        stacked = jnp.concatenate(
            [jnp.where(low_pair, pair, 0.0), jnp.where(low_pair, 0.0, pair)], axis=0
        ).astype(BF16)
        moved = jnp.dot(move, stacked, preferred_element_type=F32)
        moved = moved + pltpu.roll(moved, NFACE, 1)
        own.append(jnp.where(same_face, moved, 0.0))

    for a in range(3):
        coupled = jnp.dot(turned_rows[a], solved, preferred_element_type=F32)
        for p in range(3):
            block = -coupled[:, p * LANES : (p + 1) * LANES]
            if p == a:
                block = block + own[p]
            block = lax.dot_general(
                block.astype(BF16),
                col_moves[p],
                (((1,), (1,)), ((), ())),
                preferred_element_type=F32,
            )
            even_lanes = iota((HALF, 2 * LANES), 1) % LANES < NFACE
            for s in range(2):
                top = block[s * NFACE : s * NFACE + HALF]
                bottom = block[s * NFACE + HALF : (s + 1) * NFACE]
                merged = jnp.where(even_lanes, top, bottom).astype(BF16)
                contrib_ref[0, 2 * a + s, 2 * p] = merged[:, :LANES]
                contrib_ref[0, 2 * a + s, 2 * p + 1] = merged[:, LANES:]


def condense(inverse, to_face, to_interior, diag, cells, orient, owner):
    number = inverse.shape[0]
    grid_spec = pltpu.PrefetchScalarGridSpec(
        num_scalar_prefetch=3,
        grid=(number,),
        in_specs=[
            pl.BlockSpec((1, NINT, NINT), lambda e, cell, o, w: (e, 0, 0)),
            pl.BlockSpec((1, NINT, WIDTH), lambda e, cell, o, w: (e, 0, 0)),
            pl.BlockSpec((1, WIDTH, NINT), lambda e, cell, o, w: (e, 0, 0)),
            pl.BlockSpec((1, FACES, NFACE * NFACE), lambda e, cell, o, w: (e, 0, 0)),
        ],
        out_specs=[
            pl.BlockSpec(
                (1, FACES, FACES, HALF, LANES), lambda e, cell, o, w: (cell[e], 0, 0, 0, 0)
            ),
            pl.BlockSpec(memory_space=pltpu.SMEM),
        ],
        scratch_shapes=[pltpu.VMEM((FACES * HALF, LANES), F32)],
    )
    return pl.pallas_call(
        condense_kernel,
        grid_spec=grid_spec,
        out_shape=[
            jax.ShapeDtypeStruct((number, FACES, FACES, HALF, LANES), BF16),
            jax.ShapeDtypeStruct((F_DEV,), jnp.int32),
        ],
        compiler_params=pltpu.CompilerParams(
            dimension_semantics=("arbitrary",), vmem_limit_bytes=32 << 20
        ),
        name="condense",
    )(cells, orient, owner, inverse, to_face, to_interior, diag)


def exchange_kernel(
    counts,
    slot_ref,
    flag_ref,
    c_ref,
    out_ref,
    right,
    stage,
    landed,
    flat,
    halo_send,
    halo_recv,
    send,
    recv,
):
    n_gx, n_gy, n_gz = counts
    gx, gy, gz = lax.axis_index("gx"), lax.axis_index("gy"), lax.axis_index("gz")
    below = (
        {"gx": lax.rem(gx + n_gx - 1, n_gx)},
        {"gy": lax.rem(gy + n_gy - 1, n_gy)},
        {"gz": lax.rem(gz + n_gz - 1, n_gz)},
    )
    above = ({"gx": lax.rem(gx + 1, n_gx)}, {"gy": lax.rem(gy + 1, n_gy)})

    barrier = pltpu.get_barrier_semaphore()
    greeted = [below[0], below[1], above[0], above[1]]
    greeted += [{"gz": lax.rem(gz + k, n_gz)} for k in range(1, n_gz)]
    for device in greeted:
        pl.semaphore_signal(barrier, inc=1, device_id=device, device_id_type=MESH)
    pl.semaphore_wait(barrier, len(greeted))

    halo = []
    for d in range(3):
        source = (c_ref.at[0, :, :, 0], c_ref.at[:, 0, :, 2], c_ref.at[:, :, 0, 4])[d]
        place = (right.at[0, 1], right.at[1, :, 1], right.at[2, :, :, 1])[d]
        copy = pltpu.make_async_remote_copy(
            src_ref=source,
            dst_ref=place,
            send_sem=halo_send.at[d],
            recv_sem=halo_recv.at[d],
            device_id=below[d],
            device_id_type=MESH,
        )
        copy.start()
        halo.append(copy)

    def face_of(k, j):
        place = PER * lax.rem(gz + k, n_gz) + j
        f = slot_ref[place]
        cell, d = f // 3, f % 3
        cx, cy, cz = cell // 4, cell // 2 % 2, cell % 2
        keep = 1 - flag_ref[cx, cy, cz, d]
        return cx, cy, cz, d, keep

    def stage_left(k):
        for j in range(PER):
            cx, cy, cz, d, keep = face_of(k, j)
            scale = jnp.full((HALF, LANES), keep, jnp.int32).astype(F32).astype(BF16)
            for b in range(5):
                other = b + (b >= 2 * d + 1).astype(jnp.int32)
                stage[k, j, b] = c_ref[cx, cy, cz, 2 * d + 1, other] * scale

    diagonal = (
        iota((HALF, LANES), 1) % NFACE == 2 * iota((HALF, LANES), 0) + iota((HALF, LANES), 1) // NFACE
    ).astype(F32)

    def stage_right(k):
        for j in range(PER):
            cx, cy, cz, d, keep = face_of(k, j)
            wide = jnp.full((HALF, LANES), keep, jnp.int32).astype(F32)
            scale = wide.astype(BF16)
            total = c_ref[cx, cy, cz, 2 * d + 1, 2 * d + 1].astype(F32) + right[
                d, cx, cy, cz, 2 * d
            ].astype(F32)
            stage[k, j, 5] = (total * wide + diagonal * (1.0 - wide)).astype(BF16)
            for b in range(5):
                other = b + (b >= 2 * d).astype(jnp.int32)
                stage[k, j, 6 + b] = right[d, cx, cy, cz, other] * scale

    def push(k, part):
        first, size = ((0, 5), (5, 6))[part]
        return pltpu.make_async_remote_copy(
            src_ref=stage.at[k, :, pl.ds(first, size)],
            dst_ref=landed.at[k, :, pl.ds(first, size)],
            send_sem=send.at[k, part],
            recv_sem=recv.at[k, part],
            device_id={"gz": lax.rem(gz + k, n_gz)},
            device_id_type=MESH,
        )

    @pl.loop(1, n_gz)
    def _(k):
        stage_left(k)
        push(k, 0).start()

    stage_left(0)

    @pl.loop(0, 2)
    def _(u):
        @pl.loop(0, 2)
        def _(w):
            right[0, 0, u, w] = c_ref[1, u, w, 0]
            right[1, u, 0, w] = c_ref[u, 1, w, 2]
            right[2, u, w, 0] = c_ref[u, w, 1, 4]

    for copy in halo:
        copy.wait_recv()

    @pl.loop(1, n_gz)
    def _(k):
        stage_right(k)
        push(k, 1).start()

    stage_right(0)

    def unfold(source, k):
        start = PER * lax.rem(gz - k + n_gz, n_gz)
        for j in range(PER):
            for b in range(11):
                to = b + 1 if b < 5 else (0 if b == 5 else b)
                flat[to * HALF : (to + 1) * HALF, :] = source[k, j, b].astype(F32)
            for r in range(HALF):
                out_ref[start + j, :, r * LANES : (r + 1) * LANES] = flat[
                    pl.ds(r, 11, stride=HALF), :
                ].astype(BF16)

    unfold(stage, 0)

    @pl.loop(1, n_gz)
    def _(k):
        push(k, 0).wait_recv()
        push(k, 1).wait_recv()
        unfold(landed, k)

    @pl.loop(1, n_gz)
    def _(k):
        push(k, 0).wait_send()
        push(k, 1).wait_send()

    for copy in halo:
        copy.wait_send()


def exchange(slots, flags, contrib, counts):
    n_gz = counts[2]
    vmem = pl.BlockSpec(memory_space=pltpu.VMEM)
    smem = pl.BlockSpec(memory_space=pltpu.SMEM)

    def body(*refs):
        exchange_kernel(counts, *refs)

    return pl.pallas_call(
        body,
        out_shape=jax.ShapeDtypeStruct((F_DEV, 11, NFACE * NFACE), BF16),
        in_specs=[smem, smem, vmem],
        out_specs=vmem,
        scratch_shapes=[
            pltpu.VMEM((3, 2, 2, 2, FACES, HALF, LANES), BF16),
            pltpu.VMEM((n_gz, PER, 11, HALF, LANES), BF16),
            pltpu.VMEM((n_gz, PER, 11, HALF, LANES), BF16),
            pltpu.VMEM((16 * HALF, LANES), F32),
            pltpu.SemaphoreType.DMA((3,)),
            pltpu.SemaphoreType.DMA((3,)),
            pltpu.SemaphoreType.DMA((n_gz, 2)),
            pltpu.SemaphoreType.DMA((n_gz, 2)),
        ],
        compiler_params=pltpu.CompilerParams(
            collective_id=0, has_side_effects=True, vmem_limit_bytes=48 << 20
        ),
        name="exchange",
    )(slots, flags, contrib)


def shards(
    interior_inverse,
    interior_to_face,
    face_to_interior,
    face_diag,
    element_cell,
    face_orient,
    face_owner,
    prescribed_face_mask,
):
    contrib, slots = condense(
        interior_inverse,
        interior_to_face,
        face_to_interior,
        face_diag,
        element_cell,
        face_orient,
        face_owner,
    )
    counts = (lax.axis_size("gx"), lax.axis_size("gy"), lax.axis_size("gz"))
    contrib = contrib.reshape(2, 2, 2, FACES, FACES, HALF, LANES)
    rows = exchange(slots, prescribed_face_mask, contrib, counts)
    return rows.reshape(1, 1, F_DEV, 11, NFACE * NFACE)


def solution(mesh):
    return jax.shard_map(
        shards,
        mesh=mesh,
        in_specs=(
            P(("gx", "gy", "gz"), None, None),
            P(("gx", "gy", "gz"), None, None),
            P(("gx", "gy", "gz"), None, None),
            P(("gx", "gy", "gz"), None, None),
            P(("gx", "gy", "gz")),
            P(("gx", "gy", "gz"), None),
            P("gx", "gy", "gz", None),
            P("gx", "gy", "gz", None),
        ),
        out_specs=P("gx", "gy", "gz", None, None),
        check_vma=False,
    )
```

```python
import jax
import jax.numpy as jnp
from jax import lax
from jax.experimental import pallas as pl
from jax.experimental.pallas import tpu as pltpu
from jax.sharding import PartitionSpec as P

Q = 8
NFACE = 64
NINT = 512
FACES = 6
WIDTH = FACES * NFACE
E_DEV = 8
F_DEV = 24
PER = 3
HALF = 32
LANES = 128
MESH = pl.DeviceIdType.MESH
F32 = jnp.float32
BF16 = jnp.bfloat16


def iota(shape, axis):
    return lax.broadcasted_iota(jnp.int32, shape, axis)


def mapped_nodes(nodes, codes):
    first, second = nodes // Q, nodes % Q
    swapped = codes // 4 % 2 == 1
    new_first = jnp.where(swapped, second, first)
    new_second = jnp.where(swapped, first, second)
    new_first = jnp.where(codes % 2 == 1, Q - 1 - new_first, new_first)
    new_second = jnp.where(codes // 2 % 2 == 1, Q - 1 - new_second, new_second)
    return Q * new_first + new_second


def turn_rows(e, orient_ref, to_interior, diag_rows, own):
    lane = iota((1, LANES), 1)
    row = iota((LANES, LANES), 0)
    col = iota((LANES, LANES), 1)
    row_node = 2 * (row % HALF) + row // HALF % 2 + NFACE * (row // NFACE)
    half_nodes = 2 * (lane % HALF) + lane // NFACE
    same_face = row // NFACE == col // NFACE
    low = col[:NFACE] < NFACE
    for p in range(3):
        code_a, code_b = orient_ref[e, 2 * p], orient_ref[e, 2 * p + 1]
        second = lane // NFACE
        codes = jnp.where(second == 1, code_b, code_a)
        target = mapped_nodes(lane % NFACE, codes) + NFACE * second
        move = (target == row_node).astype(BF16)
        at = slice(p * LANES, (p + 1) * LANES)
        turned = jnp.dot(move, to_interior[e, at, :], preferred_element_type=F32)
        to_interior[e, at, :] = turned.astype(BF16)
        second = lane // HALF % 2
        codes = jnp.where(second == 1, code_b, code_a)
        target = mapped_nodes(half_nodes, codes) + NFACE * second
        move = (target == row_node).astype(BF16)
        at = pl.multiple_of(e * FACES * HALF + p * NFACE, NFACE)
        pair = diag_rows[pl.ds(at, NFACE), :]
        stacked = jnp.concatenate(
            [jnp.where(low, pair, 0.0), jnp.where(low, 0.0, pair)], axis=0
        ).astype(BF16)
        moved = jnp.dot(move, stacked, preferred_element_type=F32)
        moved = moved + pltpu.roll(moved, NFACE, 1)
        own[e, p] = jnp.where(same_face, moved, 0.0)


def pair_of_columns(e, p, orient_ref, to_interior, solved, own, contrib):
    lane = iota((1, LANES), 1)
    second = lane // NFACE
    codes = jnp.where(second == 1, orient_ref[e, 2 * p + 1], orient_ref[e, 2 * p])
    target = mapped_nodes(lane % NFACE, codes) + NFACE * second
    wide = iota((2 * LANES, LANES), 0)
    move = (target == wide % NFACE + NFACE * (wide // LANES)).astype(BF16)
    columns = solved[e, :, p * LANES : (p + 1) * LANES]
    blocks = -jnp.dot(to_interior[e], columns, preferred_element_type=F32)
    parts = [blocks[a * LANES : (a + 1) * LANES] for a in range(3)]
    parts[p] = parts[p] + own[e, p]
    blocks = lax.dot_general(
        jnp.concatenate(parts, axis=0).astype(BF16),
        move,
        (((1,), (1,)), ((), ())),
        preferred_element_type=F32,
    )
    even_lanes = iota((HALF, LANES), 1) < NFACE
    for a in range(FACES):
        top = blocks[a * NFACE : a * NFACE + HALF]
        bottom = blocks[a * NFACE + HALF : (a + 1) * NFACE]
        for q in range(2):
            at = slice(q * LANES, (q + 1) * LANES)
            contrib[e, a, 2 * p + q] = jnp.where(even_lanes, top[:, at], bottom[:, at]).astype(BF16)


RUNS = ((0, 1), (1, 2), (3, 2), (5, 6))


def condense_kernel(
    counts,
    inverse_hbm,
    to_face_hbm,
    to_interior_hbm,
    diag_hbm,
    cell_hbm,
    orient_hbm,
    owner_hbm,
    flag_hbm,
    out_ref,
    inverse,
    to_face,
    to_interior,
    diag,
    cell_ref,
    orient_ref,
    owner_ref,
    flag_ref,
    element_ref,
    slot_ref,
    solved,
    diag_rows,
    own,
    contrib,
    rim,
    right,
    stage,
    landed,
    flat,
    arrive,
    small_arrive,
    halo_send,
    halo_recv,
    send,
    recv,
):
    n_gx, n_gy, n_gz = counts
    gx, gy, gz = lax.axis_index("gx"), lax.axis_index("gy"), lax.axis_index("gz")
    below = (
        {"gx": lax.rem(gx + n_gx - 1, n_gx)},
        {"gy": lax.rem(gy + n_gy - 1, n_gy)},
        {"gz": lax.rem(gz + n_gz - 1, n_gz)},
    )
    above = ({"gx": lax.rem(gx + 1, n_gx)}, {"gy": lax.rem(gy + 1, n_gy)})

    small = [
        pltpu.make_async_copy(source, place, small_arrive.at[i])
        for i, (source, place) in enumerate(
            (
                (owner_hbm, owner_ref),
                (cell_hbm, cell_ref),
                (orient_hbm, orient_ref),
                (flag_hbm, flag_ref),
                (diag_hbm, diag),
            )
        )
    ]
    for copy in small:
        copy.start()

    def input_of(e, i):
        source, place = ((inverse_hbm, inverse), (to_face_hbm, to_face), (to_interior_hbm, to_interior))[i]
        return pltpu.make_async_copy(source.at[e], place.at[e], arrive.at[e, i])

    for e in range(E_DEV):
        for i in range(3):
            input_of(e, i).start()

    barrier = pltpu.get_barrier_semaphore()
    greeted = [below[0], below[1], above[0], above[1]]
    greeted += [{"gz": lax.rem(gz + k, n_gz)} for k in range(1, n_gz)]
    for device in greeted:
        pl.semaphore_signal(barrier, inc=1, device_id=device, device_id_type=MESH)

    for copy in small:
        copy.wait()

    @pl.loop(0, E_DEV)
    def _(c):
        found = 0
        for e in range(E_DEV):
            found = jnp.where(cell_ref[e] == c, e, found)
        element_ref[c] = found

    @pl.loop(0, F_DEV)
    def _(v):
        found = 0
        for f in range(F_DEV):
            at = (f // 12, f // 6 % 2, f // 3 % 2, f % 3)
            found = jnp.where(owner_ref[at] == v, f, found)
        slot_ref[v] = found

    for a in range(FACES):
        faces = diag[a].astype(F32)
        for r in range(HALF):
            diag_rows[pl.ds(a * HALF + r, E_DEV, stride=FACES * HALF), :] = faces[
                :, r * LANES : (r + 1) * LANES
            ]

    @pl.loop(0, E_DEV // 2)
    def _(i):
        for e in (2 * i, 2 * i + 1):
            for n in range(3):
                input_of(e, n).wait()
        for e in (2 * i, 2 * i + 1):
            product = jnp.dot(inverse[e], to_face[e], preferred_element_type=F32)
            solved[e] = product.astype(BF16)
            turn_rows(e, orient_ref, to_interior, diag_rows, own)

    def columns(p):
        @pl.loop(0, E_DEV // 2)
        def _(i):
            for e in (2 * i, 2 * i + 1):
                pair_of_columns(e, p, orient_ref, to_interior, solved, own, contrib)

    def face_of(k, j):
        f = slot_ref[PER * lax.rem(gz + k, n_gz) + j]
        cell, d = f // 3, f % 3
        cx, cy, cz = cell // 4, cell // 2 % 2, cell % 2
        keep = 1 - flag_ref[cx, cy, cz, d]
        return cell, cx, cy, cz, d, keep

    def stage_left(k, run):
        first, size = RUNS[run]
        for j in range(PER):
            cell, _, _, _, d, keep = face_of(k, j)
            e = element_ref[cell]
            scale = jnp.full((HALF, LANES), keep, jnp.int32).astype(F32).astype(BF16)
            for b in range(first, first + size):
                other = b + (b >= 2 * d + 1).astype(jnp.int32)
                stage[k, j, b] = contrib[e, 2 * d + 1, other] * scale

    diagonal = (
        iota((HALF, LANES), 1) % NFACE == 2 * iota((HALF, LANES), 0) + iota((HALF, LANES), 1) // NFACE
    ).astype(F32)

    def stage_right(k):
        for j in range(PER):
            cell, cx, cy, cz, d, keep = face_of(k, j)
            e = element_ref[cell]
            wide = jnp.full((HALF, LANES), keep, jnp.int32).astype(F32)
            scale = wide.astype(BF16)
            total = contrib[e, 2 * d + 1, 2 * d + 1].astype(F32) + right[
                d, cx, cy, cz, 2 * d
            ].astype(F32)
            stage[k, j, 5] = (total * wide + diagonal * (1.0 - wide)).astype(BF16)
            for b in range(5):
                other = b + (b >= 2 * d).astype(jnp.int32)
                stage[k, j, 6 + b] = right[d, cx, cy, cz, other] * scale

    def push(k, run):
        first, size = RUNS[run]
        return pltpu.make_async_remote_copy(
            src_ref=stage.at[k, :, pl.ds(first, size)],
            dst_ref=landed.at[k, :, pl.ds(first, size)],
            send_sem=send.at[k, run],
            recv_sem=recv.at[k, run],
            device_id={"gz": lax.rem(gz + k, n_gz)},
            device_id_type=MESH,
        )

    def send_left(run):
        @pl.loop(1, n_gz)
        def _(k):
            stage_left(k, run)
            push(k, run).start()

        stage_left(0, run)

    columns(0)
    pl.semaphore_wait(barrier, len(greeted))
    send_left(0)
    columns(1)
    send_left(1)
    columns(2)

    for d in range(3):
        step = (4, 2, 1)[d]
        free = ((2, 1), (4, 1), (4, 2))[d]

        @pl.loop(0, 2)
        def _(u):
            @pl.loop(0, 2)
            def _(w):
                cell = free[0] * u + free[1] * w
                rim[d, u, w] = contrib[element_ref[cell], 2 * d]
                at = ((0, u, w), (u, 0, w), (u, w, 0))[d]
                right[(d, *at)] = contrib[element_ref[cell + step], 2 * d]

    halo = []
    for d in range(3):
        place = (right.at[0, 1], right.at[1, :, 1], right.at[2, :, :, 1])[d]
        copy = pltpu.make_async_remote_copy(
            src_ref=rim.at[d],
            dst_ref=place,
            send_sem=halo_send.at[d],
            recv_sem=halo_recv.at[d],
            device_id=below[d],
            device_id_type=MESH,
        )
        copy.start()
        halo.append(copy)

    send_left(2)

    for copy in halo:
        copy.wait_recv()

    @pl.loop(1, n_gz)
    def _(k):
        stage_right(k)
        push(k, 3).start()

    stage_right(0)

    rows_at = 11 * HALF

    def spread(source, k, first, size):
        start = PER * lax.rem(gz - k + n_gz, n_gz)
        for j in range(PER):
            for b in range(first, first + size):
                to = b + 1 if b < 5 else (0 if b == 5 else b)
                at = pl.multiple_of((start + j) * rows_at + to * HALF, HALF)
                flat[pl.ds(at, HALF), :] = source[k, j, b].astype(F32)

    def unfold(b):
        for r in range(HALF):
            out_ref[b, :, r * LANES : (r + 1) * LANES] = flat[
                pl.ds(b * HALF + r, F_DEV, stride=rows_at), :
            ].astype(BF16)

    spread(stage, 0, 0, 11)

    @pl.loop(1, n_gz)
    def _(k):
        for run in range(3):
            push(k, run).wait_recv()
        spread(landed, k, 0, 5)

    @pl.loop(1, 6)
    def _(b):
        unfold(b)

    @pl.loop(1, n_gz)
    def _(k):
        push(k, 3).wait_recv()
        spread(landed, k, 5, 6)

    unfold(0)

    @pl.loop(6, 11)
    def _(b):
        unfold(b)

    @pl.loop(1, n_gz)
    def _(k):
        for run in range(4):
            push(k, run).wait_send()

    for copy in halo:
        copy.wait_send()


def shards(
    interior_inverse,
    interior_to_face,
    face_to_interior,
    face_diag,
    element_cell,
    face_orient,
    face_owner,
    prescribed_face_mask,
):
    counts = (lax.axis_size("gx"), lax.axis_size("gy"), lax.axis_size("gz"))
    n_gz = counts[2]
    block = (HALF, LANES)

    def body(*refs):
        condense_kernel(counts, *refs)

    rows = pl.pallas_call(
        body,
        out_shape=jax.ShapeDtypeStruct((11, F_DEV, NFACE * NFACE), BF16),
        in_specs=[pl.BlockSpec(memory_space=pl.ANY)] * 8,
        out_specs=pl.BlockSpec(memory_space=pltpu.VMEM),
        scratch_shapes=[
            pltpu.VMEM((E_DEV, NINT, NINT), BF16),
            pltpu.VMEM((E_DEV, NINT, WIDTH), BF16),
            pltpu.VMEM((E_DEV, WIDTH, NINT), BF16),
            pltpu.VMEM((FACES, E_DEV, NFACE * NFACE), BF16),
            pltpu.SMEM((E_DEV,), jnp.int32),
            pltpu.SMEM((E_DEV, FACES), jnp.int32),
            pltpu.SMEM((2, 2, 2, 3), jnp.int32),
            pltpu.SMEM((2, 2, 2, 3), jnp.int32),
            pltpu.SMEM((E_DEV,), jnp.int32),
            pltpu.SMEM((F_DEV,), jnp.int32),
            pltpu.VMEM((E_DEV, NINT, WIDTH), BF16),
            pltpu.VMEM((E_DEV * FACES * HALF, LANES), F32),
            pltpu.VMEM((E_DEV, 3, LANES, LANES), F32),
            pltpu.VMEM((E_DEV, FACES, FACES, *block), BF16),
            pltpu.VMEM((3, 2, 2, FACES, *block), BF16),
            pltpu.VMEM((3, 2, 2, 2, FACES, *block), BF16),
            pltpu.VMEM((n_gz, PER, 11, *block), BF16),
            pltpu.VMEM((n_gz, PER, 11, *block), BF16),
            pltpu.VMEM((F_DEV * 11 * HALF, LANES), F32),
            pltpu.SemaphoreType.DMA((E_DEV, 3)),
            pltpu.SemaphoreType.DMA((5,)),
            pltpu.SemaphoreType.DMA((3,)),
            pltpu.SemaphoreType.DMA((3,)),
            pltpu.SemaphoreType.DMA((n_gz, 4)),
            pltpu.SemaphoreType.DMA((n_gz, 4)),
        ],
        compiler_params=pltpu.CompilerParams(
            collective_id=0, has_side_effects=True, vmem_limit_bytes=40 << 20
        ),
        name="condense",
    )(
        *(
            pltpu.with_memory_space_constraint(value, pltpu.HBM)
            for value in (
                interior_inverse,
                interior_to_face,
                face_to_interior,
                face_diag.transpose(1, 0, 2),
                element_cell,
                face_orient,
                face_owner,
                prescribed_face_mask,
            )
        )
    )
    return rows.transpose(1, 0, 2).reshape(1, 1, F_DEV, 11, NFACE * NFACE)


def solution(mesh):
    return jax.shard_map(
        shards,
        mesh=mesh,
        in_specs=(
            P(("gx", "gy", "gz"), None, None),
            P(("gx", "gy", "gz"), None, None),
            P(("gx", "gy", "gz"), None, None),
            P(("gx", "gy", "gz"), None, None),
            P(("gx", "gy", "gz")),
            P(("gx", "gy", "gz"), None),
            P("gx", "gy", "gz", None),
            P("gx", "gy", "gz", None),
        ),
        out_specs=P("gx", "gy", "gz", None, None),
        check_vma=False,
    )
```

```python
import jax
import jax.numpy as jnp
from jax import lax
from jax.experimental import pallas as pl
from jax.experimental.pallas import tpu as pltpu
from jax.sharding import PartitionSpec as P

Q = 8
NFACE = 64
NINT = 512
FACES = 6
WIDTH = FACES * NFACE
E_DEV = 8
F_DEV = 24
PER = 3
HALF = 32
LANES = 128
MESH = pl.DeviceIdType.MESH
F32 = jnp.float32
BF16 = jnp.bfloat16


def iota(shape, axis):
    return lax.broadcasted_iota(jnp.int32, shape, axis)


def mapped_nodes(nodes, codes):
    first, second = nodes // Q, nodes % Q
    swapped = codes // 4 % 2 == 1
    new_first = jnp.where(swapped, second, first)
    new_second = jnp.where(swapped, first, second)
    new_first = jnp.where(codes % 2 == 1, Q - 1 - new_first, new_first)
    new_second = jnp.where(codes // 2 % 2 == 1, Q - 1 - new_second, new_second)
    return Q * new_first + new_second


def turn_rows(e, orient_ref, to_interior, diag_rows, own):
    lane = iota((1, LANES), 1)
    row = iota((LANES, LANES), 0)
    col = iota((LANES, LANES), 1)
    row_node = 2 * (row % HALF) + row // HALF % 2 + NFACE * (row // NFACE)
    half_nodes = 2 * (lane % HALF) + lane // NFACE
    same_face = row // NFACE == col // NFACE
    low = col[:NFACE] < NFACE
    for p in range(3):
        code_a, code_b = orient_ref[e, 2 * p], orient_ref[e, 2 * p + 1]
        second = lane // NFACE
        codes = jnp.where(second == 1, code_b, code_a)
        target = mapped_nodes(lane % NFACE, codes) + NFACE * second
        move = (target == row_node).astype(BF16)
        at = slice(p * LANES, (p + 1) * LANES)
        turned = jnp.dot(move, to_interior[e, at, :], preferred_element_type=F32)
        to_interior[e, at, :] = turned.astype(BF16)
        second = lane // HALF % 2
        codes = jnp.where(second == 1, code_b, code_a)
        target = mapped_nodes(half_nodes, codes) + NFACE * second
        move = (target == row_node).astype(BF16)
        at = pl.multiple_of(e * FACES * HALF + p * NFACE, NFACE)
        pair = diag_rows[pl.ds(at, NFACE), :]
        stacked = jnp.concatenate(
            [jnp.where(low, pair, 0.0), jnp.where(low, 0.0, pair)], axis=0
        ).astype(BF16)
        moved = jnp.dot(move, stacked, preferred_element_type=F32)
        moved = moved + pltpu.roll(moved, NFACE, 1)
        own[e, p] = jnp.where(same_face, moved, 0.0)


def turned_blocks(e, orient_ref, to_interior, solved, own, place):
    lane = iota((1, LANES), 1)
    second = lane // NFACE
    wide = iota((2 * LANES, LANES), 0)
    wide_node = wide % NFACE + NFACE * (wide // LANES)
    even_lanes = iota((HALF, LANES), 1) < NFACE
    coupled = jnp.dot(to_interior[e], solved[e], preferred_element_type=F32)
    for p in range(3):
        codes = jnp.where(second == 1, orient_ref[e, 2 * p + 1], orient_ref[e, 2 * p])
        target = mapped_nodes(lane % NFACE, codes) + NFACE * second
        move = (target == wide_node).astype(BF16)
        blocks = -coupled[:, p * LANES : (p + 1) * LANES]
        parts = [blocks[a * LANES : (a + 1) * LANES] for a in range(3)]
        parts[p] = parts[p] + own[e, p]
        blocks = lax.dot_general(
            jnp.concatenate(parts, axis=0).astype(BF16),
            move,
            (((1,), (1,)), ((), ())),
            preferred_element_type=F32,
        )
        for a in range(FACES):
            top = blocks[a * NFACE : a * NFACE + HALF]
            bottom = blocks[a * NFACE + HALF : (a + 1) * NFACE]
            for q in range(2):
                at = slice(q * LANES, (q + 1) * LANES)
                merged = jnp.where(even_lanes, top[:, at], bottom[:, at])
                place[a, 2 * p + q] = merged.astype(BF16)


RUNS = ((0, 5), (5, 6))
AHEAD = 2


def condense_kernel(
    counts,
    inverse_hbm,
    to_face_hbm,
    to_interior_hbm,
    diag_hbm,
    cell_hbm,
    orient_hbm,
    owner_hbm,
    flag_hbm,
    out_ref,
    inverse,
    to_face,
    to_interior,
    diag,
    cell_ref,
    orient_ref,
    owner_ref,
    flag_ref,
    element_ref,
    slot_ref,
    solved,
    diag_rows,
    own,
    contrib,
    right,
    stage,
    landed,
    flat,
    arrive,
    small_arrive,
    halo_send,
    halo_recv,
    send,
    recv,
):
    n_gx, n_gy, n_gz = counts
    gx, gy, gz = lax.axis_index("gx"), lax.axis_index("gy"), lax.axis_index("gz")
    below = (
        {"gx": lax.rem(gx + n_gx - 1, n_gx)},
        {"gy": lax.rem(gy + n_gy - 1, n_gy)},
        {"gz": lax.rem(gz + n_gz - 1, n_gz)},
    )
    above = ({"gx": lax.rem(gx + 1, n_gx)}, {"gy": lax.rem(gy + 1, n_gy)})

    small = [
        pltpu.make_async_copy(source, place, small_arrive.at[i])
        for i, (source, place) in enumerate(
            (
                (owner_hbm, owner_ref),
                (cell_hbm, cell_ref),
                (orient_hbm, orient_ref),
                (flag_hbm, flag_ref),
                (diag_hbm, diag),
            )
        )
    ]
    for copy in small:
        copy.start()

    def input_of(e, i):
        source, place = ((inverse_hbm, inverse), (to_face_hbm, to_face), (to_interior_hbm, to_interior))[i]
        return pltpu.make_async_copy(source.at[e], place.at[e], arrive.at[e, i])

    def fetch(i):
        for e in (2 * i, 2 * i + 1):
            for n in range(3):
                input_of(e, n).start()

    for i in range(AHEAD):
        fetch(i)

    barrier = pltpu.get_barrier_semaphore()
    greeted = [below[0], below[1], above[0], above[1]]
    greeted += [{"gz": lax.rem(gz + k, n_gz)} for k in range(1, n_gz)]
    for device in greeted:
        pl.semaphore_signal(barrier, inc=1, device_id=device, device_id_type=MESH)

    for copy in small:
        copy.wait()

    @pl.loop(0, E_DEV)
    def _(c):
        found = 0
        for e in range(E_DEV):
            found = jnp.where(cell_ref[e] == c, e, found)
        element_ref[c] = found

    for a in range(FACES):
        faces = diag[a].astype(F32)
        for r in range(HALF):
            diag_rows[pl.ds(a * HALF + r, E_DEV, stride=FACES * HALF), :] = faces[
                :, r * LANES : (r + 1) * LANES
            ]

    @pl.loop(0, E_DEV // 2)
    def _(i):
        for e in (2 * i, 2 * i + 1):
            for n in range(3):
                input_of(e, n).wait()

        @pl.when(i + AHEAD < E_DEV // 2)
        def _():
            fetch(i + AHEAD)

        for e in (2 * i, 2 * i + 1):
            product = jnp.dot(inverse[e], to_face[e], preferred_element_type=F32)
            solved[e] = product.astype(BF16)
            turn_rows(e, orient_ref, to_interior, diag_rows, own)

        for q in range(F_DEV // (E_DEV // 2)):
            v = F_DEV // (E_DEV // 2) * i + q
            found = 0
            for f in range(F_DEV):
                at = (f // 12, f // 6 % 2, f // 3 % 2, f % 3)
                found = jnp.where(owner_ref[at] == v, f, found)
            slot_ref[v] = found

    def halo(d, i):
        cy, cz = lax.rem(i, 2), i // 2
        source, place = (
            (contrib.at[0, cy, cz, 0], right.at[0, 1, cy, cz]),
            (contrib.at[:, cy, cz, 2], right.at[1, :, 1, cz]),
            (contrib.at[:, cy, cz, 4], right.at[2, :, cy, 1]),
        )[d]
        return pltpu.make_async_remote_copy(
            src_ref=source,
            dst_ref=place,
            send_sem=halo_send.at[d, i],
            recv_sem=halo_recv.at[d, i],
            device_id=below[d],
            device_id_type=MESH,
        )

    def each_halo(i, act):
        @pl.when(lax.rem(i, 2) == 0)
        def _():
            act(halo(1, i))

        @pl.when(i // 2 == 0)
        def _():
            act(halo(2, i))

        act(halo(0, i))

    pl.semaphore_wait(barrier, len(greeted))

    @pl.loop(0, E_DEV // 2)
    def _(i):
        cy, cz = lax.rem(i, 2), i // 2
        for cx in range(2):
            e = element_ref[4 * cx + 2 * cy + cz]
            place = contrib.at[cx, cy, cz]
            turned_blocks(e, orient_ref, to_interior, solved, own, place)
        each_halo(i, lambda copy: copy.start())

    def face_of(k, j):
        f = slot_ref[PER * lax.rem(gz + k, n_gz) + j]
        cell, d = f // 3, f % 3
        cx, cy, cz = cell // 4, cell // 2 % 2, cell % 2
        keep = 1 - flag_ref[cx, cy, cz, d]
        return cx, cy, cz, d, keep

    def stage_left(k, run):
        first, size = RUNS[run]
        for j in range(PER):
            cx, cy, cz, d, keep = face_of(k, j)
            scale = jnp.full((HALF, LANES), keep, jnp.int32).astype(F32).astype(BF16)
            for b in range(first, first + size):
                other = b + (b >= 2 * d + 1).astype(jnp.int32)
                stage[k, j, b] = contrib[cx, cy, cz, 2 * d + 1, other] * scale

    diagonal = (
        iota((HALF, LANES), 1) % NFACE == 2 * iota((HALF, LANES), 0) + iota((HALF, LANES), 1) // NFACE
    ).astype(F32)

    def stage_right(k):
        for j in range(PER):
            cx, cy, cz, d, keep = face_of(k, j)
            wide = jnp.full((HALF, LANES), keep, jnp.int32).astype(F32)
            scale = wide.astype(BF16)
            total = contrib[cx, cy, cz, 2 * d + 1, 2 * d + 1].astype(F32) + right[
                d, cx, cy, cz, 2 * d
            ].astype(F32)
            stage[k, j, 5] = (total * wide + diagonal * (1.0 - wide)).astype(BF16)
            for b in range(5):
                other = b + (b >= 2 * d).astype(jnp.int32)
                stage[k, j, 6 + b] = right[d, cx, cy, cz, other] * scale

    def push(k, run):
        first, size = RUNS[run]
        return pltpu.make_async_remote_copy(
            src_ref=stage.at[k, :, pl.ds(first, size)],
            dst_ref=landed.at[k, :, pl.ds(first, size)],
            send_sem=send.at[k, run],
            recv_sem=recv.at[k, run],
            device_id={"gz": lax.rem(gz + k, n_gz)},
            device_id_type=MESH,
        )

    def send_left(run):
        @pl.loop(1, n_gz)
        def _(k):
            stage_left(k, run)
            push(k, run).start()

        stage_left(0, run)

    send_left(0)

    @pl.loop(0, 2)
    def _(u):
        @pl.loop(0, 2)
        def _(w):
            right[0, 0, u, w] = contrib[1, u, w, 0]
            right[1, u, 0, w] = contrib[u, 1, w, 2]
            right[2, u, w, 0] = contrib[u, w, 1, 4]

    @pl.loop(0, E_DEV // 2)
    def _(i):
        each_halo(i, lambda copy: copy.wait_recv())

    @pl.loop(1, n_gz)
    def _(k):
        stage_right(k)
        push(k, 1).start()

    stage_right(0)

    rows_at = 11 * HALF

    def spread(source, k, first, size):
        start = PER * lax.rem(gz - k + n_gz, n_gz)
        for j in range(PER):
            for b in range(first, first + size):
                to = b + 1 if b < 5 else (0 if b == 5 else b)
                at = pl.multiple_of((start + j) * rows_at + to * HALF, HALF)
                flat[pl.ds(at, HALF), :] = source[k, j, b].astype(F32)

    def unfold(b, first, count):
        for r in range(HALF):
            out_ref[b, pl.ds(first, count), r * LANES : (r + 1) * LANES] = flat[
                pl.ds(first * rows_at + b * HALF + r, count, stride=rows_at), :
            ].astype(BF16)

    spread(stage, 0, 0, 11)

    @pl.loop(1, n_gz)
    def _(k):
        push(k, 0).wait_recv()
        spread(landed, k, 0, 5)

    @pl.loop(1, 6)
    def _(b):
        unfold(b, 0, F_DEV)

    done = 0
    for source in range(n_gz):
        k = lax.rem(gz - source + n_gz, n_gz)

        @pl.when(k != 0)
        def _():
            push(k, 1).wait_recv()
            spread(landed, k, 5, 6)

        ready = (source + 1) * PER // 8 * 8
        if ready > done:

            @pl.loop(5, 11)
            def _(b, done=done, ready=ready):
                unfold(jnp.where(b == 5, 0, b), done, ready - done)

            done = ready

    @pl.loop(1, n_gz)
    def _(k):
        for run in range(2):
            push(k, run).wait_send()

    @pl.loop(0, E_DEV // 2)
    def _(i):
        each_halo(i, lambda copy: copy.wait_send())


def shards(
    interior_inverse,
    interior_to_face,
    face_to_interior,
    face_diag,
    element_cell,
    face_orient,
    face_owner,
    prescribed_face_mask,
):
    counts = (lax.axis_size("gx"), lax.axis_size("gy"), lax.axis_size("gz"))
    n_gz = counts[2]
    block = (HALF, LANES)

    def body(*refs):
        condense_kernel(counts, *refs)

    rows = pl.pallas_call(
        body,
        out_shape=jax.ShapeDtypeStruct((11, F_DEV, NFACE * NFACE), BF16),
        in_specs=[pl.BlockSpec(memory_space=pl.ANY)] * 8,
        out_specs=pl.BlockSpec(memory_space=pltpu.VMEM),
        scratch_shapes=[
            pltpu.VMEM((E_DEV, NINT, NINT), BF16),
            pltpu.VMEM((E_DEV, NINT, WIDTH), BF16),
            pltpu.VMEM((E_DEV, WIDTH, NINT), BF16),
            pltpu.VMEM((FACES, E_DEV, NFACE * NFACE), BF16),
            pltpu.SMEM((E_DEV,), jnp.int32),
            pltpu.SMEM((E_DEV, FACES), jnp.int32),
            pltpu.SMEM((2, 2, 2, 3), jnp.int32),
            pltpu.SMEM((2, 2, 2, 3), jnp.int32),
            pltpu.SMEM((E_DEV,), jnp.int32),
            pltpu.SMEM((F_DEV,), jnp.int32),
            pltpu.VMEM((E_DEV, NINT, WIDTH), BF16),
            pltpu.VMEM((E_DEV * FACES * HALF, LANES), F32),
            pltpu.VMEM((E_DEV, 3, LANES, LANES), F32),
            pltpu.VMEM((2, 2, 2, FACES, FACES, *block), BF16),
            pltpu.VMEM((3, 2, 2, 2, FACES, *block), BF16),
            pltpu.VMEM((n_gz, PER, 11, *block), BF16),
            pltpu.VMEM((n_gz, PER, 11, *block), BF16),
            pltpu.VMEM((F_DEV * 11 * HALF, LANES), F32),
            pltpu.SemaphoreType.DMA((E_DEV, 3)),
            pltpu.SemaphoreType.DMA((5,)),
            pltpu.SemaphoreType.DMA((3, E_DEV // 2)),
            pltpu.SemaphoreType.DMA((3, E_DEV // 2)),
            pltpu.SemaphoreType.DMA((n_gz, 2)),
            pltpu.SemaphoreType.DMA((n_gz, 2)),
        ],
        compiler_params=pltpu.CompilerParams(
            collective_id=0, has_side_effects=True, vmem_limit_bytes=40 << 20
        ),
        name="condense",
    )(
        *(
            pltpu.with_memory_space_constraint(value, pltpu.HBM)
            for value in (
                interior_inverse,
                interior_to_face,
                face_to_interior,
                face_diag.transpose(1, 0, 2),
                element_cell,
                face_orient,
                face_owner,
                prescribed_face_mask,
            )
        )
    )
    return rows.transpose(1, 0, 2).reshape(1, 1, F_DEV, 11, NFACE * NFACE)


def solution(mesh):
    return jax.shard_map(
        shards,
        mesh=mesh,
        in_specs=(
            P(("gx", "gy", "gz"), None, None),
            P(("gx", "gy", "gz"), None, None),
            P(("gx", "gy", "gz"), None, None),
            P(("gx", "gy", "gz"), None, None),
            P(("gx", "gy", "gz")),
            P(("gx", "gy", "gz"), None),
            P("gx", "gy", "gz", None),
            P("gx", "gy", "gz", None),
        ),
        out_specs=P("gx", "gy", "gz", None, None),
        check_vma=False,
    )
```

```python
import jax
import jax.numpy as jnp
from jax import lax
from jax.experimental import pallas as pl
from jax.experimental.pallas import tpu as pltpu
from jax.sharding import PartitionSpec as P

Q = 8
NFACE = 64
NINT = 512
FACES = 6
WIDTH = FACES * NFACE
E_DEV = 8
F_DEV = 24
PER = 3
HALF = 32
LANES = 128
MESH = pl.DeviceIdType.MESH
F32 = jnp.float32
BF16 = jnp.bfloat16


def iota(shape, axis):
    return lax.broadcasted_iota(jnp.int32, shape, axis)


def mapped_nodes(nodes, codes):
    first, second = nodes // Q, nodes % Q
    swapped = codes // 4 % 2 == 1
    new_first = jnp.where(swapped, second, first)
    new_second = jnp.where(swapped, first, second)
    new_first = jnp.where(codes % 2 == 1, Q - 1 - new_first, new_first)
    new_second = jnp.where(codes // 2 % 2 == 1, Q - 1 - new_second, new_second)
    return Q * new_first + new_second


def turn_rows(e, orient_ref, to_interior, diag_rows, own):
    lane = iota((1, LANES), 1)
    row = iota((LANES, LANES), 0)
    col = iota((LANES, LANES), 1)
    row_node = 2 * (row % HALF) + row // HALF % 2 + NFACE * (row // NFACE)
    half_nodes = 2 * (lane % HALF) + lane // NFACE
    same_face = row // NFACE == col // NFACE
    low = col[:NFACE] < NFACE
    for p in range(3):
        code_a, code_b = orient_ref[e, 2 * p], orient_ref[e, 2 * p + 1]
        second = lane // NFACE
        codes = jnp.where(second == 1, code_b, code_a)
        target = mapped_nodes(lane % NFACE, codes) + NFACE * second
        move = (target == row_node).astype(BF16)
        at = slice(p * LANES, (p + 1) * LANES)
        turned = jnp.dot(move, to_interior[e, at, :], preferred_element_type=F32)
        to_interior[e, at, :] = turned.astype(BF16)
        second = lane // HALF % 2
        codes = jnp.where(second == 1, code_b, code_a)
        target = mapped_nodes(half_nodes, codes) + NFACE * second
        move = (target == row_node).astype(BF16)
        at = pl.multiple_of(e * FACES * HALF + p * NFACE, NFACE)
        pair = diag_rows[pl.ds(at, NFACE), :]
        stacked = jnp.concatenate(
            [jnp.where(low, pair, 0.0), jnp.where(low, 0.0, pair)], axis=0
        ).astype(BF16)
        moved = jnp.dot(move, stacked, preferred_element_type=F32)
        moved = moved + pltpu.roll(moved, NFACE, 1)
        own[e, p] = jnp.where(same_face, moved, 0.0)


def turned_blocks(e, orient_ref, to_interior, solved, own, place):
    lane = iota((1, LANES), 1)
    second = lane // NFACE
    wide = iota((2 * LANES, LANES), 0)
    wide_node = wide % NFACE + NFACE * (wide // LANES)
    even_lanes = iota((HALF, LANES), 1) < NFACE
    coupled = jnp.dot(to_interior[e], solved[e], preferred_element_type=F32)
    for p in range(3):
        codes = jnp.where(second == 1, orient_ref[e, 2 * p + 1], orient_ref[e, 2 * p])
        target = mapped_nodes(lane % NFACE, codes) + NFACE * second
        move = (target == wide_node).astype(BF16)
        blocks = -coupled[:, p * LANES : (p + 1) * LANES]
        parts = [blocks[a * LANES : (a + 1) * LANES] for a in range(3)]
        parts[p] = parts[p] + own[e, p]
        blocks = lax.dot_general(
            jnp.concatenate(parts, axis=0).astype(BF16),
            move,
            (((1,), (1,)), ((), ())),
            preferred_element_type=F32,
        )
        for a in range(FACES):
            top = blocks[a * NFACE : a * NFACE + HALF]
            bottom = blocks[a * NFACE + HALF : (a + 1) * NFACE]
            for q in range(2):
                at = slice(q * LANES, (q + 1) * LANES)
                merged = jnp.where(even_lanes, top[:, at], bottom[:, at])
                place[a, 2 * p + q] = merged.astype(BF16)


RUNS = ((0, 5), (5, 6))
CELLS_AT = 32
AHEAD = 2


def condense_kernel(
    counts,
    inverse_hbm,
    to_face_hbm,
    to_interior_hbm,
    diag_hbm,
    cell_hbm,
    orient_hbm,
    owner_hbm,
    flag_hbm,
    out_ref,
    inverse,
    to_face,
    to_interior,
    diag,
    cell_ref,
    orient_ref,
    owner_ref,
    flag_ref,
    table_ref,
    table,
    solved,
    diag_rows,
    own,
    contrib,
    right,
    stage,
    landed,
    flat,
    arrive,
    small_arrive,
    halo_send,
    halo_recv,
    send,
    recv,
    table_sem,
):
    n_gx, n_gy, n_gz = counts
    gx, gy, gz = lax.axis_index("gx"), lax.axis_index("gy"), lax.axis_index("gz")
    below = (
        {"gx": lax.rem(gx + n_gx - 1, n_gx)},
        {"gy": lax.rem(gy + n_gy - 1, n_gy)},
        {"gz": lax.rem(gz + n_gz - 1, n_gz)},
    )
    above = ({"gx": lax.rem(gx + 1, n_gx)}, {"gy": lax.rem(gy + 1, n_gy)})

    small = [
        pltpu.make_async_copy(source, place, small_arrive.at[i])
        for i, (source, place) in enumerate(
            (
                (owner_hbm, owner_ref),
                (cell_hbm, cell_ref),
                (orient_hbm, orient_ref),
                (flag_hbm, flag_ref),
                (diag_hbm, diag),
            )
        )
    ]
    for copy in small:
        copy.start()

    def input_of(e, i):
        source, place = ((inverse_hbm, inverse), (to_face_hbm, to_face), (to_interior_hbm, to_interior))[i]
        return pltpu.make_async_copy(source.at[e], place.at[e], arrive.at[e, i])

    def fetch(i):
        for e in (2 * i, 2 * i + 1):
            for n in range(3):
                input_of(e, n).start()

    for i in range(AHEAD):
        fetch(i)

    barrier = pltpu.get_barrier_semaphore()
    greeted = [below[0], below[1], above[0], above[1]]
    greeted += [{"gz": lax.rem(gz + k, n_gz)} for k in range(1, n_gz)]
    for device in greeted:
        pl.semaphore_signal(barrier, inc=1, device_id=device, device_id_type=MESH)

    for copy in small:
        copy.wait()

    at = iota((1, LANES), 1)
    found = jnp.zeros((1, LANES), jnp.int32)
    for f in range(F_DEV):
        owner = owner_ref[f // 12, f // 6 % 2, f // 3 % 2, f % 3]
        found = jnp.where(at == owner, f, found)
    for e in range(E_DEV):
        found = jnp.where(at == CELLS_AT + cell_ref[e], e, found)
    table[...] = found
    table_copy = pltpu.make_async_copy(table, table_ref, table_sem)
    table_copy.start()

    for a in range(FACES):
        faces = diag[a].astype(F32)
        for r in range(HALF):
            diag_rows[pl.ds(a * HALF + r, E_DEV, stride=FACES * HALF), :] = faces[
                :, r * LANES : (r + 1) * LANES
            ]

    @pl.loop(0, E_DEV // 2)
    def _(i):
        for e in (2 * i, 2 * i + 1):
            for n in range(3):
                input_of(e, n).wait()

        @pl.when(i + AHEAD < E_DEV // 2)
        def _():
            fetch(i + AHEAD)

        for e in (2 * i, 2 * i + 1):
            product = jnp.dot(inverse[e], to_face[e], preferred_element_type=F32)
            solved[e] = product.astype(BF16)
            turn_rows(e, orient_ref, to_interior, diag_rows, own)

    table_copy.wait()

    def halo(d, i):
        cy, cz = lax.rem(i, 2), i // 2
        source, place = (
            (contrib.at[0, cy, cz, 0], right.at[0, 1, cy, cz]),
            (contrib.at[:, cy, cz, 2], right.at[1, :, 1, cz]),
            (contrib.at[:, cy, cz, 4], right.at[2, :, cy, 1]),
        )[d]
        return pltpu.make_async_remote_copy(
            src_ref=source,
            dst_ref=place,
            send_sem=halo_send.at[d, i],
            recv_sem=halo_recv.at[d, i],
            device_id=below[d],
            device_id_type=MESH,
        )

    def each_halo(i, act):
        @pl.when(i // 2 == 0)
        def _():
            act(halo(2, i))

        @pl.when(lax.rem(i, 2) == 0)
        def _():
            act(halo(1, i))

        act(halo(0, i))


    pl.semaphore_wait(barrier, len(greeted))

    @pl.loop(0, E_DEV // 2)
    def _(i):
        cy, cz = lax.rem(i, 2), i // 2
        for cx in range(2):
            e = table_ref[0, CELLS_AT + 4 * cx + 2 * cy + cz]
            place = contrib.at[cx, cy, cz]
            turned_blocks(e, orient_ref, to_interior, solved, own, place)
        each_halo(i, lambda copy: copy.start())

    def face_of(k, j):
        f = table_ref[0, PER * lax.rem(gz + k, n_gz) + j]
        cell, d = f // 3, f % 3
        cx, cy, cz = cell // 4, cell // 2 % 2, cell % 2
        keep = 1 - flag_ref[cx, cy, cz, d]
        return cx, cy, cz, d, keep

    def stage_left(k, run):
        first, size = RUNS[run]
        for j in range(PER):
            cx, cy, cz, d, keep = face_of(k, j)
            scale = jnp.full((HALF, LANES), keep, jnp.int32).astype(F32).astype(BF16)
            for b in range(first, first + size):
                other = b + (b >= 2 * d + 1).astype(jnp.int32)
                stage[k, j, b] = contrib[cx, cy, cz, 2 * d + 1, other] * scale

    diagonal = (
        iota((HALF, LANES), 1) % NFACE == 2 * iota((HALF, LANES), 0) + iota((HALF, LANES), 1) // NFACE
    ).astype(F32)

    def stage_right(k):
        for j in range(PER):
            cx, cy, cz, d, keep = face_of(k, j)
            wide = jnp.full((HALF, LANES), keep, jnp.int32).astype(F32)
            scale = wide.astype(BF16)
            total = contrib[cx, cy, cz, 2 * d + 1, 2 * d + 1].astype(F32) + right[
                d, cx, cy, cz, 2 * d
            ].astype(F32)
            stage[k, j, 5] = (total * wide + diagonal * (1.0 - wide)).astype(BF16)
            for b in range(5):
                other = b + (b >= 2 * d).astype(jnp.int32)
                stage[k, j, 6 + b] = right[d, cx, cy, cz, other] * scale

    def push(k, run):
        first, size = RUNS[run]
        return pltpu.make_async_remote_copy(
            src_ref=stage.at[k, :, pl.ds(first, size)],
            dst_ref=landed.at[k, :, pl.ds(first, size)],
            send_sem=send.at[k, run],
            recv_sem=recv.at[k, run],
            device_id={"gz": lax.rem(gz + k, n_gz)},
            device_id_type=MESH,
        )

    def send_left(run):
        @pl.loop(1, n_gz)
        def _(q):
            k = jnp.where(lax.rem(gz, 2) == 1, n_gz - q, q)
            stage_left(k, run)
            push(k, run).start()

        stage_left(0, run)

    send_left(0)

    @pl.loop(0, 2)
    def _(u):
        @pl.loop(0, 2)
        def _(w):
            right[0, 0, u, w] = contrib[1, u, w, 0]
            right[1, u, 0, w] = contrib[u, 1, w, 2]
            right[2, u, w, 0] = contrib[u, w, 1, 4]

    @pl.loop(0, E_DEV // 2)
    def _(i):
        each_halo(i, lambda copy: copy.wait_recv())

    @pl.loop(1, n_gz)
    def _(q):
        k = jnp.where(lax.rem(gz, 2) == 1, n_gz - q, q)
        stage_right(k)
        push(k, 1).start()

    stage_right(0)

    rows_at = 11 * HALF

    def spread(source, k, first, size):
        start = PER * lax.rem(gz - k + n_gz, n_gz)
        for j in range(PER):
            for b in range(first, first + size):
                to = b + 1 if b < 5 else (0 if b == 5 else b)
                at = pl.multiple_of((start + j) * rows_at + to * HALF, HALF)
                flat[pl.ds(at, HALF), :] = source[k, j, b].astype(F32)

    def unfold(b, first, count):
        for r in range(HALF):
            out_ref[b, pl.ds(first, count), r * LANES : (r + 1) * LANES] = flat[
                pl.ds(first * rows_at + b * HALF + r, count, stride=rows_at), :
            ].astype(BF16)

    spread(stage, 0, 0, 11)

    @pl.loop(1, n_gz)
    def _(k):
        push(k, 0).wait_recv()
        spread(landed, k, 0, 5)

    @pl.loop(1, 6)
    def _(b):
        unfold(b, 0, F_DEV)

    done = 0
    for source in range(n_gz):
        k = lax.rem(gz - source + n_gz, n_gz)

        @pl.when(k != 0)
        def _():
            push(k, 1).wait_recv()
            spread(landed, k, 5, 6)

        ready = (source + 1) * PER // 8 * 8
        if ready > done:

            @pl.loop(5, 11)
            def _(b, done=done, ready=ready):
                unfold(jnp.where(b == 5, 0, b), done, ready - done)

            done = ready

    @pl.loop(1, n_gz)
    def _(k):
        for run in range(2):
            push(k, run).wait_send()

    @pl.loop(0, E_DEV // 2)
    def _(i):
        each_halo(i, lambda copy: copy.wait_send())


def shards(
    interior_inverse,
    interior_to_face,
    face_to_interior,
    face_diag,
    element_cell,
    face_orient,
    face_owner,
    prescribed_face_mask,
):
    counts = (lax.axis_size("gx"), lax.axis_size("gy"), lax.axis_size("gz"))
    n_gz = counts[2]
    block = (HALF, LANES)

    def body(*refs):
        condense_kernel(counts, *refs)

    rows = pl.pallas_call(
        body,
        out_shape=jax.ShapeDtypeStruct((11, F_DEV, NFACE * NFACE), BF16),
        in_specs=[pl.BlockSpec(memory_space=pl.ANY)] * 8,
        out_specs=pl.BlockSpec(memory_space=pltpu.VMEM),
        scratch_shapes=[
            pltpu.VMEM((E_DEV, NINT, NINT), BF16),
            pltpu.VMEM((E_DEV, NINT, WIDTH), BF16),
            pltpu.VMEM((E_DEV, WIDTH, NINT), BF16),
            pltpu.VMEM((FACES, E_DEV, NFACE * NFACE), BF16),
            pltpu.SMEM((E_DEV,), jnp.int32),
            pltpu.SMEM((E_DEV, FACES), jnp.int32),
            pltpu.SMEM((2, 2, 2, 3), jnp.int32),
            pltpu.SMEM((2, 2, 2, 3), jnp.int32),
            pltpu.SMEM((1, LANES), jnp.int32),
            pltpu.VMEM((1, LANES), jnp.int32),
            pltpu.VMEM((E_DEV, NINT, WIDTH), BF16),
            pltpu.VMEM((E_DEV * FACES * HALF, LANES), F32),
            pltpu.VMEM((E_DEV, 3, LANES, LANES), F32),
            pltpu.VMEM((2, 2, 2, FACES, FACES, *block), BF16),
            pltpu.VMEM((3, 2, 2, 2, FACES, *block), BF16),
            pltpu.VMEM((n_gz, PER, 11, *block), BF16),
            pltpu.VMEM((n_gz, PER, 11, *block), BF16),
            pltpu.VMEM((F_DEV * 11 * HALF, LANES), F32),
            pltpu.SemaphoreType.DMA((E_DEV, 3)),
            pltpu.SemaphoreType.DMA((5,)),
            pltpu.SemaphoreType.DMA((3, E_DEV // 2)),
            pltpu.SemaphoreType.DMA((3, E_DEV // 2)),
            pltpu.SemaphoreType.DMA((n_gz, 2)),
            pltpu.SemaphoreType.DMA((n_gz, 2)),
            pltpu.SemaphoreType.DMA,
        ],
        compiler_params=pltpu.CompilerParams(
            collective_id=0, has_side_effects=True, vmem_limit_bytes=40 << 20
        ),
        name="condense",
    )(
        *(
            pltpu.with_memory_space_constraint(value, pltpu.HBM)
            for value in (
                interior_inverse,
                interior_to_face,
                face_to_interior,
                face_diag.transpose(1, 0, 2),
                element_cell,
                face_orient,
                face_owner,
                prescribed_face_mask,
            )
        )
    )
    return rows.transpose(1, 0, 2).reshape(1, 1, F_DEV, 11, NFACE * NFACE)


def solution(mesh):
    return jax.shard_map(
        shards,
        mesh=mesh,
        in_specs=(
            P(("gx", "gy", "gz"), None, None),
            P(("gx", "gy", "gz"), None, None),
            P(("gx", "gy", "gz"), None, None),
            P(("gx", "gy", "gz"), None, None),
            P(("gx", "gy", "gz")),
            P(("gx", "gy", "gz"), None),
            P("gx", "gy", "gz", None),
            P("gx", "gy", "gz", None),
        ),
        out_specs=P("gx", "gy", "gz", None, None),
        check_vma=False,
    )
```

```python
import jax
import jax.numpy as jnp
from jax import lax
from jax.experimental import pallas as pl
from jax.experimental.pallas import tpu as pltpu
from jax.sharding import PartitionSpec as P

Q = 8
NFACE = 64
NINT = 512
FACES = 6
WIDTH = FACES * NFACE
E_DEV = 8
F_DEV = 24
PER = 3
HALF = 32
LANES = 128
MESH = pl.DeviceIdType.MESH
F32 = jnp.float32
BF16 = jnp.bfloat16


def iota(shape, axis):
    return lax.broadcasted_iota(jnp.int32, shape, axis)


def mapped_nodes(nodes, codes):
    first, second = nodes // Q, nodes % Q
    swapped = codes // 4 % 2 == 1
    new_first = jnp.where(swapped, second, first)
    new_second = jnp.where(swapped, first, second)
    new_first = jnp.where(codes % 2 == 1, Q - 1 - new_first, new_first)
    new_second = jnp.where(codes // 2 % 2 == 1, Q - 1 - new_second, new_second)
    return Q * new_first + new_second


def turn_rows(e, orient_ref, to_interior, diag_rows, own):
    lane = iota((1, LANES), 1)
    row = iota((LANES, LANES), 0)
    col = iota((LANES, LANES), 1)
    row_node = 2 * (row % HALF) + row // HALF % 2 + NFACE * (row // NFACE)
    half_nodes = 2 * (lane % HALF) + lane // NFACE
    same_face = row // NFACE == col // NFACE
    low = col[:NFACE] < NFACE
    for p in range(3):
        code_a, code_b = orient_ref[e, 2 * p], orient_ref[e, 2 * p + 1]
        second = lane // NFACE
        codes = jnp.where(second == 1, code_b, code_a)
        target = mapped_nodes(lane % NFACE, codes) + NFACE * second
        move = (target == row_node).astype(BF16)
        at = slice(p * LANES, (p + 1) * LANES)
        turned = jnp.dot(move, to_interior[e, at, :], preferred_element_type=F32)
        to_interior[e, at, :] = turned.astype(BF16)
        second = lane // HALF % 2
        codes = jnp.where(second == 1, code_b, code_a)
        target = mapped_nodes(half_nodes, codes) + NFACE * second
        move = (target == row_node).astype(BF16)
        at = pl.multiple_of(e * FACES * HALF + p * NFACE, NFACE)
        pair = diag_rows[pl.ds(at, NFACE), :]
        stacked = jnp.concatenate(
            [jnp.where(low, pair, 0.0), jnp.where(low, 0.0, pair)], axis=0
        ).astype(BF16)
        moved = jnp.dot(move, stacked, preferred_element_type=F32)
        moved = moved + pltpu.roll(moved, NFACE, 1)
        own[e, p] = jnp.where(same_face, moved, 0.0)


def turned_blocks(e, orient_ref, to_interior, solved, own, place):
    lane = iota((1, LANES), 1)
    second = lane // NFACE
    wide = iota((2 * LANES, LANES), 0)
    wide_node = wide % NFACE + NFACE * (wide // LANES)
    even_lanes = iota((HALF, LANES), 1) < NFACE
    coupled = lax.dot_general(
        to_interior[e], solved[e], (((1,), (1,)), ((), ())), preferred_element_type=F32
    )
    for p in range(3):
        codes = jnp.where(second == 1, orient_ref[e, 2 * p + 1], orient_ref[e, 2 * p])
        target = mapped_nodes(lane % NFACE, codes) + NFACE * second
        move = (target == wide_node).astype(BF16)
        blocks = -coupled[:, p * LANES : (p + 1) * LANES]
        parts = [blocks[a * LANES : (a + 1) * LANES] for a in range(3)]
        parts[p] = parts[p] + own[e, p]
        blocks = lax.dot_general(
            jnp.concatenate(parts, axis=0).astype(BF16),
            move,
            (((1,), (1,)), ((), ())),
            preferred_element_type=F32,
        )
        for a in range(FACES):
            top = blocks[a * NFACE : a * NFACE + HALF]
            bottom = blocks[a * NFACE + HALF : (a + 1) * NFACE]
            for q in range(2):
                at = slice(q * LANES, (q + 1) * LANES)
                merged = jnp.where(even_lanes, top[:, at], bottom[:, at])
                place[a, 2 * p + q] = merged.astype(BF16)


RUNS = ((0, 5), (5, 6))
CELLS_AT = 32
AHEAD = 2


def condense_kernel(
    counts,
    inverse_hbm,
    to_face_hbm,
    to_interior_hbm,
    diag_hbm,
    cell_hbm,
    orient_hbm,
    owner_hbm,
    flag_hbm,
    out_ref,
    inverse,
    to_face,
    to_interior,
    diag,
    cell_ref,
    orient_ref,
    owner_ref,
    flag_ref,
    table_ref,
    table,
    solved,
    diag_rows,
    own,
    contrib,
    right,
    stage,
    landed,
    flat,
    arrive,
    small_arrive,
    halo_send,
    halo_recv,
    send,
    recv,
    table_sem,
):
    n_gx, n_gy, n_gz = counts
    gx, gy, gz = lax.axis_index("gx"), lax.axis_index("gy"), lax.axis_index("gz")
    below = (
        {"gx": lax.rem(gx + n_gx - 1, n_gx)},
        {"gy": lax.rem(gy + n_gy - 1, n_gy)},
        {"gz": lax.rem(gz + n_gz - 1, n_gz)},
    )
    above = ({"gx": lax.rem(gx + 1, n_gx)}, {"gy": lax.rem(gy + 1, n_gy)})

    small = [
        pltpu.make_async_copy(source, place, small_arrive.at[i])
        for i, (source, place) in enumerate(
            (
                (owner_hbm, owner_ref),
                (cell_hbm, cell_ref),
                (orient_hbm, orient_ref),
                (flag_hbm, flag_ref),
                (diag_hbm, diag),
            )
        )
    ]
    for copy in small:
        copy.start()

    def input_of(e, i):
        source, place = ((inverse_hbm, inverse), (to_face_hbm, to_face), (to_interior_hbm, to_interior))[i]
        return pltpu.make_async_copy(source.at[e], place.at[e], arrive.at[e, i])

    def fetch(i):
        for e in (2 * i, 2 * i + 1):
            for n in range(3):
                input_of(e, n).start()

    fetch(0)

    barrier = pltpu.get_barrier_semaphore()
    greeted = [below[0], below[1], above[0], above[1]]
    greeted += [{"gz": lax.rem(gz + k, n_gz)} for k in range(1, n_gz)]
    for device in greeted:
        pl.semaphore_signal(barrier, inc=1, device_id=device, device_id_type=MESH)

    for copy in small:
        copy.wait()

    at = iota((1, LANES), 1)
    found = jnp.zeros((1, LANES), jnp.int32)
    for f in range(F_DEV):
        owner = owner_ref[f // 12, f // 6 % 2, f // 3 % 2, f % 3]
        found = jnp.where(at == owner, f, found)
    for e in range(E_DEV):
        found = jnp.where(at == CELLS_AT + cell_ref[e], e, found)
    table[...] = found
    table_copy = pltpu.make_async_copy(table, table_ref, table_sem)
    table_copy.start()

    for a in range(FACES):
        faces = diag[a].astype(F32)
        for r in range(HALF):
            diag_rows[pl.ds(a * HALF + r, E_DEV, stride=FACES * HALF), :] = faces[
                :, r * LANES : (r + 1) * LANES
            ]

    for i in range(1, AHEAD):
        fetch(i)

    @pl.loop(0, E_DEV // 2)
    def _(i):
        for e in (2 * i, 2 * i + 1):
            for n in range(3):
                input_of(e, n).wait()

        @pl.when(i + AHEAD < E_DEV // 2)
        def _():
            fetch(i + AHEAD)

        for e in (2 * i, 2 * i + 1):
            product = lax.dot_general(
                to_face[e], inverse[e], (((0,), (1,)), ((), ())), preferred_element_type=F32
            )
            solved[e] = product.astype(BF16)
            turn_rows(e, orient_ref, to_interior, diag_rows, own)

    table_copy.wait()

    def halo(d, i):
        cy, cz = lax.rem(i, 2), i // 2
        source, place = (
            (contrib.at[0, cy, cz, 0], right.at[0, 1, cy, cz]),
            (contrib.at[:, cy, cz, 2], right.at[1, :, 1, cz]),
            (contrib.at[:, cy, cz, 4], right.at[2, :, cy, 1]),
        )[d]
        return pltpu.make_async_remote_copy(
            src_ref=source,
            dst_ref=place,
            send_sem=halo_send.at[d, i],
            recv_sem=halo_recv.at[d, i],
            device_id=below[d],
            device_id_type=MESH,
        )

    def each_halo(i, act):
        @pl.when(i // 2 == 0)
        def _():
            act(halo(2, i))

        @pl.when(lax.rem(i, 2) == 0)
        def _():
            act(halo(1, i))

        act(halo(0, i))


    pl.semaphore_wait(barrier, len(greeted))

    @pl.loop(0, E_DEV // 2)
    def _(i):
        cy, cz = lax.rem(i, 2), i // 2
        for cx in range(2):
            e = table_ref[0, CELLS_AT + 4 * cx + 2 * cy + cz]
            place = contrib.at[cx, cy, cz]
            turned_blocks(e, orient_ref, to_interior, solved, own, place)
        each_halo(i, lambda copy: copy.start())

    def face_of(k, j):
        f = table_ref[0, PER * lax.rem(gz + k, n_gz) + j]
        cell, d = f // 3, f % 3
        cx, cy, cz = cell // 4, cell // 2 % 2, cell % 2
        keep = 1 - flag_ref[cx, cy, cz, d]
        return cx, cy, cz, d, keep

    def stage_left(k, run):
        first, size = RUNS[run]
        for j in range(PER):
            cx, cy, cz, d, keep = face_of(k, j)
            scale = jnp.full((HALF, LANES), keep, jnp.int32).astype(F32).astype(BF16)
            for b in range(first, first + size):
                other = b + (b >= 2 * d + 1).astype(jnp.int32)
                stage[k, j, b] = contrib[cx, cy, cz, 2 * d + 1, other] * scale

    diagonal = (
        iota((HALF, LANES), 1) % NFACE == 2 * iota((HALF, LANES), 0) + iota((HALF, LANES), 1) // NFACE
    ).astype(F32)

    def stage_right(k):
        for j in range(PER):
            cx, cy, cz, d, keep = face_of(k, j)
            wide = jnp.full((HALF, LANES), keep, jnp.int32).astype(F32)
            scale = wide.astype(BF16)
            total = contrib[cx, cy, cz, 2 * d + 1, 2 * d + 1].astype(F32) + right[
                d, cx, cy, cz, 2 * d
            ].astype(F32)
            stage[k, j, 5] = (total * wide + diagonal * (1.0 - wide)).astype(BF16)
            for b in range(5):
                other = b + (b >= 2 * d).astype(jnp.int32)
                stage[k, j, 6 + b] = right[d, cx, cy, cz, other] * scale

    def push(k, run):
        first, size = RUNS[run]
        return pltpu.make_async_remote_copy(
            src_ref=stage.at[k, :, pl.ds(first, size)],
            dst_ref=landed.at[k, :, pl.ds(first, size)],
            send_sem=send.at[k, run],
            recv_sem=recv.at[k, run],
            device_id={"gz": lax.rem(gz + k, n_gz)},
            device_id_type=MESH,
        )

    def send_left(run):
        @pl.loop(1, n_gz)
        def _(q):
            k = jnp.where(lax.rem(gz, 2) == 1, n_gz - q, q)
            stage_left(k, run)
            push(k, run).start()

        stage_left(0, run)

    send_left(0)

    @pl.loop(0, 2)
    def _(u):
        @pl.loop(0, 2)
        def _(w):
            right[0, 0, u, w] = contrib[1, u, w, 0]
            right[1, u, 0, w] = contrib[u, 1, w, 2]
            right[2, u, w, 0] = contrib[u, w, 1, 4]

    @pl.loop(0, E_DEV // 2)
    def _(i):
        each_halo(i, lambda copy: copy.wait_recv())

    @pl.loop(1, n_gz)
    def _(q):
        k = jnp.where(lax.rem(gz, 2) == 1, n_gz - q, q)
        stage_right(k)
        push(k, 1).start()

    stage_right(0)

    rows_at = 11 * HALF

    def spread(source, k, first, size):
        start = PER * lax.rem(gz - k + n_gz, n_gz)
        for j in range(PER):
            for b in range(first, first + size):
                to = b + 1 if b < 5 else (0 if b == 5 else b)
                at = pl.multiple_of((start + j) * rows_at + to * HALF, HALF)
                flat[pl.ds(at, HALF), :] = source[k, j, b].astype(F32)

    def unfold(b, first, count):
        for r in range(HALF):
            out_ref[b, pl.ds(first, count), r * LANES : (r + 1) * LANES] = flat[
                pl.ds(first * rows_at + b * HALF + r, count, stride=rows_at), :
            ].astype(BF16)

    spread(stage, 0, 0, 11)

    @pl.loop(1, n_gz)
    def _(k):
        push(k, 0).wait_recv()
        spread(landed, k, 0, 5)

    @pl.loop(1, 6)
    def _(b):
        unfold(b, 0, F_DEV)

    done = 0
    for source in range(n_gz):
        k = lax.rem(gz - source + n_gz, n_gz)

        @pl.when(k != 0)
        def _():
            push(k, 1).wait_recv()
            spread(landed, k, 5, 6)

        ready = (source + 1) * PER // 8 * 8
        if ready > done:

            @pl.loop(5, 11)
            def _(b, done=done, ready=ready):
                unfold(jnp.where(b == 5, 0, b), done, ready - done)

            done = ready

    @pl.loop(1, n_gz)
    def _(k):
        for run in range(2):
            push(k, run).wait_send()

    @pl.loop(0, E_DEV // 2)
    def _(i):
        each_halo(i, lambda copy: copy.wait_send())


def shards(
    interior_inverse,
    interior_to_face,
    face_to_interior,
    face_diag,
    element_cell,
    face_orient,
    face_owner,
    prescribed_face_mask,
):
    counts = (lax.axis_size("gx"), lax.axis_size("gy"), lax.axis_size("gz"))
    n_gz = counts[2]
    block = (HALF, LANES)

    def body(*refs):
        condense_kernel(counts, *refs)

    rows = pl.pallas_call(
        body,
        out_shape=jax.ShapeDtypeStruct((11, F_DEV, NFACE * NFACE), BF16),
        in_specs=[pl.BlockSpec(memory_space=pl.ANY)] * 8,
        out_specs=pl.BlockSpec(memory_space=pltpu.VMEM),
        scratch_shapes=[
            pltpu.VMEM((E_DEV, NINT, NINT), BF16),
            pltpu.VMEM((E_DEV, NINT, WIDTH), BF16),
            pltpu.VMEM((E_DEV, WIDTH, NINT), BF16),
            pltpu.VMEM((FACES, E_DEV, NFACE * NFACE), BF16),
            pltpu.SMEM((E_DEV,), jnp.int32),
            pltpu.SMEM((E_DEV, FACES), jnp.int32),
            pltpu.SMEM((2, 2, 2, 3), jnp.int32),
            pltpu.SMEM((2, 2, 2, 3), jnp.int32),
            pltpu.SMEM((1, LANES), jnp.int32),
            pltpu.VMEM((1, LANES), jnp.int32),
            pltpu.VMEM((E_DEV, WIDTH, NINT), BF16),
            pltpu.VMEM((E_DEV * FACES * HALF, LANES), F32),
            pltpu.VMEM((E_DEV, 3, LANES, LANES), F32),
            pltpu.VMEM((2, 2, 2, FACES, FACES, *block), BF16),
            pltpu.VMEM((3, 2, 2, 2, FACES, *block), BF16),
            pltpu.VMEM((n_gz, PER, 11, *block), BF16),
            pltpu.VMEM((n_gz, PER, 11, *block), BF16),
            pltpu.VMEM((F_DEV * 11 * HALF, LANES), F32),
            pltpu.SemaphoreType.DMA((E_DEV, 3)),
            pltpu.SemaphoreType.DMA((5,)),
            pltpu.SemaphoreType.DMA((3, E_DEV // 2)),
            pltpu.SemaphoreType.DMA((3, E_DEV // 2)),
            pltpu.SemaphoreType.DMA((n_gz, 2)),
            pltpu.SemaphoreType.DMA((n_gz, 2)),
            pltpu.SemaphoreType.DMA,
        ],
        compiler_params=pltpu.CompilerParams(
            collective_id=0, has_side_effects=True, vmem_limit_bytes=40 << 20
        ),
        name="condense",
    )(
        *(
            pltpu.with_memory_space_constraint(value, pltpu.HBM)
            for value in (
                interior_inverse,
                interior_to_face,
                face_to_interior,
                face_diag.transpose(1, 0, 2),
                element_cell,
                face_orient,
                face_owner,
                prescribed_face_mask,
            )
        )
    )
    return rows.transpose(1, 0, 2).reshape(1, 1, F_DEV, 11, NFACE * NFACE)


def solution(mesh):
    return jax.shard_map(
        shards,
        mesh=mesh,
        in_specs=(
            P(("gx", "gy", "gz"), None, None),
            P(("gx", "gy", "gz"), None, None),
            P(("gx", "gy", "gz"), None, None),
            P(("gx", "gy", "gz"), None, None),
            P(("gx", "gy", "gz")),
            P(("gx", "gy", "gz"), None),
            P("gx", "gy", "gz", None),
            P("gx", "gy", "gz", None),
        ),
        out_specs=P("gx", "gy", "gz", None, None),
        check_vma=False,
    )
```
